128 devices in a mesh: expert: 16 (over z, x), group: 8 (over y, core).
Axes of the slice: x: 4, y: 4, z: 4, core: 2. Of those that a mesh axis runs over, the one named last changes fastest.
Arguments:
- activations: bfloat16 [16384, 2048], P(('expert', 'group')), may hold values from -24 to 24
- out_grad: bfloat16 [16384, 2048], P(('expert', 'group')), may hold values from -24 to 24
- combine_weights: bfloat16 [16384, 4], P(('expert', 'group')), may hold values from 0.099609375 to 0.5
- expert_ids: int32 [16384, 4], P(('expert', 'group')), may hold values from 0 to 15, all different within a row; in each aligned block of 128 rows (0 to 127, 128 to 255, ...) at most 96 rows name the same one
- gate_up_weight: bfloat16 [16, 2048, 1024], P('expert'), may hold values from -0.125 to 0.125
- down_weight: bfloat16 [16, 2048, 512], P('expert'), may hold values from -0.25 to 0.25
Outputs:
- grad_input: bfloat16 [16384, 2048], P(('expert', 'group'))
- grad_combine: bfloat16 [16384, 4], P(('expert', 'group'))
- grad_gate_up: float32 [16, 2048, 1024], P('expert', 'group')
- grad_down: float32 [16, 2048, 512], P('expert', 'group')
The draws below stay inside these ranges and needn't reach their ends.
Inputs may be any that keep to these rules, and one draw needn't show every extreme that they name: `expert_ids`: each row names 4 different experts. Within the 128 rows of one device no expert is named more than 96 times, and in some device's rows an expert is named exactly 96 times.
All inputs are finite; a program needn't handle non-finite values.
Results may differ from the reference program's by a relative error of at most 0.0064.
Values may be sent and summed in bfloat16 or wider, within the bound.
A program may use at most 128 MiB of HBM per device.

```python
import math
import jax
import jax.numpy as jnp
import numpy as np
from jax import lax

D = 2048
FF = 512
TOP = 4
TOK_DEV = 128
EXPERTS = 16
MOST = 96
TOKENS = 16384
N_EXPERT = 16
N_GROUP = 8


def with_spikes(drawn, stream_key, source, target, parts, factor):
    def block_of(position):
        return (jnp.arange(drawn.shape[position]) // (drawn.shape[position] // parts)).reshape((-1,) + (1,) * (drawn.ndim - 1 - position))

    near = jax.random.permutation(stream_key, parts)[block_of(target)]
    far = (block_of(target) + parts // 2) % parts
    return jnp.where((block_of(source) == near) | (block_of(source) == far), factor * drawn, drawn)


def shard_levels(stream_key, extent, shards, least, largest):
    level, own = 1.0, jax.random.fold_in(stream_key, 6)
    for position, blocks in shards:
        draws = jnp.exp(jax.random.uniform(jax.random.fold_in(own, position), (blocks,), jnp.float32, least / len(shards), largest / len(shards)))
        level = level * jnp.repeat(draws, extent[position] // blocks).reshape([-1 if axis == position else 1 for axis in range(len(extent))])
    return level


def deal_out(stream_key, own, number, rows, number_of, top, limit, skew):
    sequence = jax.random.permutation(stream_key, number_of)
    crowded, ordinary = portions_of(number_of, rows * top, limit, skew, True), portions_of(number_of, rows * top, limit, skew, False)
    places = jnp.arange(number_of)

    def named(tallies, turn):
        used = int((tallies > 0).sum())
        fixed = max(1, used // 4)
        moved = fixed + (places - fixed + turn * (used - fixed)) % max(1, number_of - fixed)
        return jnp.zeros((number_of,), jnp.int32).at[sequence[jnp.where(places < fixed, places, moved)]].set(jnp.asarray(tallies, jnp.int32))

    tallies = jnp.where(number % 4 == 0, named(crowded, number // 4), named(ordinary, number - number // 4 - 1))
    mixed = jax.random.permutation(jax.random.fold_in(own, 3), number_of)
    donor, receiver = mixed[0:number_of // 2 * 2:2], mixed[1:number_of // 2 * 2:2]
    slack = jnp.minimum(tallies[donor] - 1, limit - tallies[receiver]) // 2
    slack = jnp.where((donor == sequence[0]) | (receiver == sequence[0]) | (tallies[receiver] == 0), 0, jnp.maximum(slack, 0))
    moved = jax.random.randint(jax.random.fold_in(own, 4), (number_of // 2,), 0, 1 << 20) % (slack + 1)
    tallies = tallies.at[donor].add(-moved).at[receiver].add(moved)
    items = jnp.searchsorted(jnp.cumsum(tallies), jnp.arange(rows * top), side="right").astype(jnp.int32)
    listing = items.reshape(top, rows).T
    listing = listing[jax.random.permutation(jax.random.fold_in(own, 1), rows)]
    turn = jax.random.randint(jax.random.fold_in(own, 2), (rows, 1), 0, top)
    return jnp.take_along_axis(listing, (jnp.arange(top)[None, :] + turn) % top, axis=1)


def portions_of(amount, total, most, skew, full):
    portions = [(1 << 20) // math.isqrt(rank ** skew) + 1 for rank in range(1, amount + 1)]
    largest = most if full else min(most, max(-(-total // amount), total * portions[0] // sum(portions)))
    least = 1 if total - largest >= amount - 1 else 0
    given, surplus = [largest] + [least] * (amount - 1), total - largest - least * (amount - 1)
    while surplus > 0:
        candidates = [i for i in range(1, amount) if given[i] < largest] or [i for i in range(1, amount) if given[i] < most]
        pool, left = sum([portions[i] for i in candidates]), surplus
        for i in candidates:
            extra = min(most - given[i], max(1, left * portions[i] // pool), surplus)
            given[i] = given[i] + extra
            surplus = surplus - extra
    return np.array(given)


def centred(own_key, shape, spread, most, shards=(), kind=jnp.bfloat16):
    level = shard_levels(own_key, shape, shards, -0.22, 0.18) if shards else 1.0
    values = jax.random.normal(own_key, shape, jnp.float32) * spread * level
    return jnp.minimum(jnp.maximum(values, -most), most).astype(kind)


def bell_draw_with(key, shape, deviation, most, shards, heavy, held_as=jnp.bfloat16):
    result = deviation * jax.random.normal(key, shape, jnp.float32)
    if shards:
        result = result * shard_levels(key, shape, shards, -0.22, 0.18)
    return jnp.clip(with_spikes(result, jax.random.fold_in(key, 3), *heavy), -most, most).astype(held_as)


def setup_inputs(seed: int = 0) -> dict:
    splits = jax.random.split(jax.random.key(seed), 7)
    activations = bell_draw_with(splits[0], (TOKENS, D), 1.0, 24.0, ((0, 128),), (0, 1, 128, 5.5))
    out_grad = bell_draw_with(splits[1], (TOKENS, D), 1.0, 24.0, ((0, 128),), (0, 1, 128, 5.5))
    combine_weights = jnp.clip(0.099609375 + 0.40039062 * jax.random.uniform(splits[2], (TOKENS, TOP), jnp.float32) ** shard_levels(splits[2], (TOKENS, TOP), ((0, 128),), -0.2, 0.2), 0.099609375, 0.5).astype(jnp.bfloat16)
    expert_ids_keys = jax.random.split(jax.random.fold_in(splits[3], 1), TOKENS // TOK_DEV)
    expert_ids_turns = jax.random.permutation(jax.random.fold_in(splits[3], 3), TOKENS // TOK_DEV)
    expert_ids = jax.vmap(lambda own, number: deal_out(jax.random.fold_in(splits[3], 2), own, number, TOK_DEV, EXPERTS, TOP, MOST, 2))(expert_ids_keys, expert_ids_turns).reshape((TOKENS, TOP))
    gate_up_weight = centred(splits[4], (EXPERTS, D, 2 * FF), D ** -0.5, 0.125, ((0, 16),))
    down_weight = centred(splits[5], (EXPERTS, D, FF), FF ** -0.5, 0.25, ((0, 16),))
    return dict(activations=activations, out_grad=out_grad, combine_weights=combine_weights, expert_ids=expert_ids, gate_up_weight=gate_up_weight, down_weight=down_weight)


def reference(activations, out_grad, combine_weights, expert_ids, gate_up_weight, down_weight):
    assign_total = TOKENS * TOP
    bound = N_EXPERT * N_GROUP * MOST
    flat_ids = expert_ids.reshape(-1).astype(jnp.int32)
    order = jnp.argsort(flat_ids, stable=True).astype(jnp.int32)
    columns = jnp.arange(EXPERTS, dtype=jnp.int32)
    loads = jnp.sum((flat_ids[:, None] == columns[None, :]).astype(jnp.int32), axis=0).astype(jnp.int32)
    offsets = (jnp.cumsum(loads) - loads).astype(jnp.int32)
    order_pad = jnp.concatenate([order, jnp.full((bound,), assign_total, jnp.int32)])
    act_pad = jnp.concatenate([activations, jnp.zeros((1, D), activations.dtype)], axis=0)
    grad_pad = jnp.concatenate([out_grad, jnp.zeros((1, D), out_grad.dtype)], axis=0)
    weight_pad = jnp.concatenate([combine_weights.reshape(-1).astype(jnp.float32), jnp.zeros((1,), jnp.float32)])

    def per_expert(carry, expert):
        slot_store, prob_store = carry
        picked = lax.dynamic_slice_in_dim(order_pad, offsets[expert], bound)
        live = jnp.arange(bound, dtype=jnp.int32) < loads[expert]
        assign = jnp.where(live, picked, assign_total).astype(jnp.int32)
        token_row = (assign // TOP).astype(jnp.int32)
        rows_x = act_pad[token_row].astype(jnp.float32)
        rows_g = grad_pad[token_row].astype(jnp.float32)
        rows_w = weight_pad[assign]
        weight_gu = gate_up_weight[expert].astype(jnp.float32)
        weight_down = down_weight[expert].astype(jnp.float32)
        pre = jnp.dot(rows_x, weight_gu, preferred_element_type=jnp.float32)
        gate = pre[:, :FF]
        upper = pre[:, FF:]
        sig = jax.nn.sigmoid(gate)
        hidden = (jax.nn.silu(gate) * upper).astype(jnp.bfloat16).astype(jnp.float32)
        expert_out = jnp.dot(hidden, weight_down.T, preferred_element_type=jnp.float32)
        prob_grad = jnp.sum(rows_g * expert_out, axis=1)
        scaled = (rows_w[:, None] * rows_g).astype(jnp.bfloat16).astype(jnp.float32)
        hidden_grad = jnp.dot(scaled, weight_down, preferred_element_type=jnp.float32)
        gate_grad = hidden_grad * upper * sig * (1.0 + gate * (1.0 - sig))
        upper_grad = hidden_grad * gate * sig
        pre_grad = jnp.concatenate([gate_grad, upper_grad], axis=1).astype(jnp.bfloat16).astype(jnp.float32)
        slot_grad = jnp.dot(pre_grad, weight_gu.T, preferred_element_type=jnp.float32).astype(jnp.bfloat16)
        grad_gu = jnp.dot(rows_x.T, pre_grad, preferred_element_type=jnp.float32)
        grad_dn = jnp.dot(scaled.T, hidden, preferred_element_type=jnp.float32)
        slot_store = slot_store.at[assign].set(slot_grad)
        prob_store = prob_store.at[assign].set(prob_grad)
        return (slot_store, prob_store), (grad_gu, grad_dn)

    start = (jnp.zeros((assign_total + 1, D), jnp.bfloat16), jnp.zeros((assign_total + 1,), jnp.float32))
    (slot_store, prob_store), (grad_gate_up, grad_down) = lax.scan(per_expert, start, jnp.arange(EXPERTS, dtype=jnp.int32))
    per_assign = slot_store[:assign_total].reshape(TOKENS, TOP, D).astype(jnp.float32)
    grad_input = jnp.sum(per_assign, axis=1).astype(jnp.bfloat16)
    grad_combine = prob_store[:assign_total].reshape(TOKENS, TOP).astype(jnp.bfloat16)
    return grad_input, grad_combine, grad_gate_up, grad_down
```

```python
import jax
import jax.numpy as jnp
from jax import lax
from jax.sharding import PartitionSpec as P


def body(activations, out_grad, combine_weights, expert_ids, gate_up_weight, down_weight):
    experts_all = lax.axis_size("expert")
    me = lax.axis_index("expert")
    columns = jnp.arange(experts_all, dtype=jnp.int32)
    named = expert_ids[:, :, None] == columns[None, None, :]
    table = jnp.sum(
        jnp.where(named, combine_weights.astype(jnp.float32)[:, :, None], 0.0), axis=1
    ).astype(jnp.bfloat16)
    rows_x = lax.all_gather(activations, "expert", axis=0, tiled=True)
    rows_g = lax.all_gather(out_grad, "expert", axis=0, tiled=True)
    tables = lax.all_gather(table, "expert", axis=0, tiled=True)
    mine = (columns == me).astype(jnp.float32)
    rows_w = jnp.sum(tables.astype(jnp.float32) * mine[None, :], axis=1, keepdims=True)
    weight_gu = gate_up_weight[0]
    weight_down = down_weight[0]
    hidden_dim = weight_down.shape[1]
    pre = jnp.dot(rows_x, weight_gu, preferred_element_type=jnp.float32)
    gate = pre[:, :hidden_dim]
    upper = pre[:, hidden_dim:]
    sig = jax.nn.sigmoid(gate)
    hidden = (gate * sig * upper).astype(jnp.bfloat16).astype(jnp.float32)
    raw = jnp.dot(rows_g, weight_down, preferred_element_type=jnp.float32)
    prob = jnp.sum(hidden * raw, axis=1, keepdims=True)
    hidden_grad = raw * rows_w
    gate_grad = hidden_grad * upper * sig * (1.0 + gate * (1.0 - sig))
    upper_grad = hidden_grad * gate * sig
    pre_grad = jnp.concatenate([gate_grad, upper_grad], axis=1).astype(jnp.bfloat16)
    scaled = (hidden * rows_w).astype(jnp.bfloat16)
    slot_grad = lax.dot_general(
        pre_grad, weight_gu, (((1,), (1,)), ((), ())), preferred_element_type=jnp.float32
    ).astype(jnp.bfloat16)
    grad_input = lax.psum_scatter(slot_grad, "expert", scatter_dimension=0, tiled=True)
    probs = lax.psum_scatter(
        (prob * mine[None, :]).astype(jnp.bfloat16), "expert", scatter_dimension=0, tiled=True
    )
    grad_combine = jnp.sum(
        jnp.where(named, probs.astype(jnp.float32)[:, None, :], 0.0), axis=2
    ).astype(jnp.bfloat16)
    grad_gate_up = lax.psum_scatter(
        lax.dot_general(
            rows_x, pre_grad, (((0,), (0,)), ((), ())), preferred_element_type=jnp.float32
        ).astype(jnp.bfloat16),
        "group",
        scatter_dimension=0,
        tiled=True,
    ).astype(jnp.float32)
    grad_down = lax.psum_scatter(
        lax.dot_general(
            rows_g, scaled, (((0,), (0,)), ((), ())), preferred_element_type=jnp.float32
        ).astype(jnp.bfloat16),
        "group",
        scatter_dimension=0,
        tiled=True,
    ).astype(jnp.float32)
    return (grad_input, grad_combine, grad_gate_up[None], grad_down[None])


def solution(mesh):
    rows = P(("expert", "group"), None)
    return jax.shard_map(
        body,
        mesh=mesh,
        in_specs=(rows, rows, rows, rows, P("expert", None, None), P("expert", None, None)),
        out_specs=(rows, rows, P("expert", "group", None), P("expert", "group", None)),
        check_vma=False,
    )
```

```python
import functools

import jax
import jax.numpy as jnp
from jax import lax
from jax.experimental import pallas as pl
from jax.experimental.pallas import tpu as pltpu
from jax.sharding import PartitionSpec as P

MESH = pl.DeviceIdType.MESH
LANES = 128
ORDER = (1, 3, 2, 0)
PLACE = {offset: place for place, offset in enumerate(ORDER)}
F32 = jnp.float32
BF16 = jnp.bfloat16


def kernel(
    x_in, g_in, table_in, gu_in, down_in,
    input_out, prob_out, weight_out,
    rows, gu, down, turned, pre_grad, part,
    half_in, full_in, last_half, last_full,
    give, take, ring_half, ring_full,
    local_sem, gather_send, gather_recv, half_send, half_recv, full_send, full_recv,
    last_half_send, last_half_recv, last_full_send, last_full_recv,
    give_send, give_recv, ring_half_send, ring_half_recv, ring_full_send, ring_full_recv,
):
    tok, dim = x_in.shape
    hid = down_in.shape[1]
    half = tok // 2
    group = 4 * tok
    tile = hid // 2
    feat = dim // 8
    e, q = lax.axis_index("expert"), lax.axis_index("group")
    z, x, y, c = e // 4, e % 4, q // 2, q % 2
    a, b = (1 - c) * x + c * z, (1 - c) * z + c * x
    sa, sb = 1 + 3 * c, 4 - 3 * c

    def dev_a(step):
        return (((a + step + 4) % 4) * sa + b * sb, q)

    def dev_b(step):
        return (a * sa + ((b + step + 4) % 4) * sb, q)

    def dev_y(step):
        return (e, ((y + step + 4) % 4) * 2 + c)

    other = (e, y * 2 + 1 - c)

    def remote(src, dst, send, recv, dev):
        return pltpu.make_async_remote_copy(
            src_ref=src, dst_ref=dst, send_sem=send, recv_sem=recv, device_id=dev, device_id_type=MESH
        )

    def piece(da, db, h):
        return rows.at[pl.ds(PLACE[da] * group + db * tok + h * half, half), :]

    def pass_on(src, dst, h, dev):
        da, db = dst
        return remote(piece(*src, h), piece(da, db, h), gather_send.at[da, db, h], gather_recv.at[da, db, h], dev)

    def arrived(da, db, h):
        pass_on((da, db), (da, db), h, other).wait_recv()

    def along_b(da):
        for k in range(2):
            pass_on((da, 0), (da, 1), k, dev_b(-1)).start()
            pass_on((da, 0), (da, 3), 1 - k, dev_b(1)).start()

    def onward_b(da):
        arrived(da, 1, 0)
        pass_on((da, 1), (da, 2), 0, dev_b(-1)).start()
        arrived(da, 3, 1)
        pass_on((da, 3), (da, 2), 1, dev_b(1)).start()

    def rest_of(da):
        arrived(da, 1, 1)
        arrived(da, 3, 0)
        arrived(da, 2, 0)
        arrived(da, 2, 1)

    def share(da, db, h=None):
        start = PLACE[da] * group + db * tok
        if h is None:
            return part.at[pl.ds(start, tok), :]
        return part.at[pl.ds(start + h * half, half), :]

    def add_into(dst, *srcs):
        total = dst[...].astype(F32)
        for src in srcs:
            total = total + src[...].astype(F32)
        dst[...] = total.astype(dst.dtype)

    def half_copy(da, k):
        dev = dev_b(1) if k == 0 else dev_b(-1)
        return remote(share(da, 2, k), half_in.at[da, k], half_send.at[da, k], half_recv.at[da, k], dev)

    def full_copy(da, k):
        dev = dev_b(1) if k == 0 else dev_b(-1)
        return remote(share(da, 1 + 2 * k), full_in.at[da, k], full_send.at[da, k], full_recv.at[da, k], dev)

    def last_half_copy(k):
        dev = dev_a(1) if k == 0 else dev_a(-1)
        return remote(share(2, 0, k), last_half.at[k], last_half_send.at[k], last_half_recv.at[k], dev)

    def last_full_copy(k):
        dev = dev_a(1) if k == 0 else dev_a(-1)
        return remote(share(1 + 2 * k, 0), last_full.at[k], last_full_send.at[k], last_full_recv.at[k], dev)

    def send_halves(da):
        for k in range(2):
            half_copy(da, k).start()

    def send_fulls(da):
        for k in range(2):
            half_copy(da, k).wait_recv()
            add_into(share(da, 1 + 2 * k, k), half_in.at[da, k])
            full_copy(da, k).start()

    def settle(da):
        for k in range(2):
            full_copy(da, k).wait_recv()
        add_into(share(da, 0), full_in.at[da, 0], full_in.at[da, 1])

    def column(r0):
        table = rows[pl.ds(r0, group), pl.ds(2 * dim, LANES)].astype(F32)
        lane = lax.broadcasted_iota(jnp.int32, (group, LANES), 1)
        return jnp.sum(jnp.where(lane == e, table, 0.0), axis=1, keepdims=True)

    def forward(da):
        r0 = PLACE[da] * group
        weight = column(r0)

        def step(n, prob):
            n0 = pl.multiple_of(n * tile, tile)
            n1 = pl.multiple_of(hid + n * tile, tile)
            n2 = pl.multiple_of(2 * hid + n * tile, tile)
            xs = rows[pl.ds(r0, group), pl.ds(0, dim)]
            gate = jnp.dot(xs, gu[:, pl.ds(n0, tile)], preferred_element_type=F32)
            upper = jnp.dot(xs, gu[:, pl.ds(n1, tile)], preferred_element_type=F32)
            raw = jnp.dot(
                rows[pl.ds(r0, group), pl.ds(dim, dim)], down[:, pl.ds(n0, tile)], preferred_element_type=F32
            )
            sig = jax.nn.sigmoid(gate)
            silu = gate * sig
            hidden = (silu * upper).astype(BF16).astype(F32)
            grad = raw * weight
            gate_grad = (grad * upper * sig * (1.0 + gate * (1.0 - sig))).astype(BF16)
            upper_grad = (grad * silu).astype(BF16)
            pre_grad[:, pl.ds(n0, tile)] = gate_grad
            pre_grad[:, pl.ds(n1, tile)] = upper_grad
            turned[pl.ds(n0, tile), pl.ds(r0, group)] = gate_grad.T
            turned[pl.ds(n1, tile), pl.ds(r0, group)] = upper_grad.T
            turned[pl.ds(n2, tile), pl.ds(r0, group)] = (hidden * weight).astype(BF16).T
            return prob + jnp.sum(hidden * raw, axis=1, keepdims=True)

        prob = lax.fori_loop(0, 2, step, jnp.zeros((group, 1), F32))
        lane = lax.broadcasted_iota(jnp.int32, (group, LANES), 1)
        part[pl.ds(r0, group), pl.ds(dim, LANES)] = jnp.where(lane == e, prob, 0.0).astype(BF16)

    def backward(da):
        r0 = PLACE[da] * group
        wide = dim // 4

        @pl.loop(0, 4)
        def _(m):
            m0 = pl.multiple_of(m * wide, wide)
            part[pl.ds(r0, group), pl.ds(m0, wide)] = lax.dot_general(
                pre_grad[...], gu[pl.ds(m0, wide), :], (((1,), (1,)), ((), ())), preferred_element_type=F32
            ).astype(BF16)

    def weight_block(dy, core, put):
        f0 = (((y + dy) % 4) * 2 + core) * feat

        @pl.loop(0, 3)
        def _(i):
            i0 = pl.multiple_of(i * hid, hid)
            lane = pl.multiple_of(f0 + dim * (i // 2), feat)
            put(i0, jnp.dot(turned[pl.ds(i0, hid), :], rows[:, pl.ds(lane, feat)], preferred_element_type=F32))

    def give_copy(dy):
        return remote(give.at[dy], take.at[dy], give_send.at[dy], give_recv.at[dy], other)

    high = 3 * hid // 2

    def ring_half_copy(k):
        dev = dev_y(1) if k == 0 else dev_y(-1)
        return remote(
            take.at[2, pl.ds(k * high, high), :], ring_half.at[k], ring_half_send.at[k], ring_half_recv.at[k], dev
        )

    def ring_full_copy(k):
        dev = dev_y(1) if k == 0 else dev_y(-1)
        return remote(take.at[1 + 2 * k], ring_full.at[k], ring_full_send.at[k], ring_full_recv.at[k], dev)

    def weight_grad(dy):
        def put_give(i0, value):
            give[dy, pl.ds(i0, hid), :] = value.astype(BF16)

        weight_block(dy, 1 - c, put_give)
        give_copy(dy).start()

        def put_own(i0, value):
            weight_out[pl.ds(i0, hid), :] = value

        weight_block(dy, c, put_own)
        give_copy(dy).wait_recv()
        if dy == 0:
            weight_out[...] = weight_out[...] + take[0].astype(F32)
            return
        take[dy] = (weight_out[...] + take[dy].astype(F32)).astype(BF16)
        if dy == 2:
            for k in range(2):
                ring_half_copy(k).start()
        else:
            k = dy // 2
            ring_half_copy(k).wait_recv()
            add_into(take.at[dy, pl.ds(k * high, high), :], ring_half.at[k])
            ring_full_copy(k).start()

    own = pl.ds(PLACE[0] * group, tok)
    mine = [
        pltpu.make_async_copy(x_in, rows.at[own, pl.ds(0, dim)], local_sem.at[0]),
        pltpu.make_async_copy(g_in, rows.at[own, pl.ds(dim, dim)], local_sem.at[1]),
        pltpu.make_async_copy(table_in, rows.at[own, pl.ds(2 * dim, LANES)], local_sem.at[2]),
    ]
    weights = [
        pltpu.make_async_copy(gu_in, gu, local_sem.at[3]),
        pltpu.make_async_copy(down_in, down, local_sem.at[4]),
    ]
    for copy in mine + weights:
        copy.start()
    barrier = pltpu.get_barrier_semaphore()
    for dev in (dev_a(1), dev_a(-1), dev_b(1), dev_b(-1), dev_y(1), dev_y(-1), other):
        pl.semaphore_signal(barrier, inc=1, device_id=dev, device_id_type=MESH)
    pl.semaphore_wait(barrier, 7)
    for copy in mine:
        copy.wait()

    for k in range(2):
        pass_on((0, 0), (1, 0), k, dev_a(-1)).start()
        pass_on((0, 0), (3, 0), 1 - k, dev_a(1)).start()
    arrived(1, 0, 0)
    pass_on((1, 0), (2, 0), 0, dev_a(-1)).start()
    arrived(3, 0, 1)
    pass_on((3, 0), (2, 0), 1, dev_a(1)).start()
    arrived(1, 0, 1)
    along_b(1)
    arrived(3, 0, 0)
    onward_b(1)
    along_b(3)
    for copy in weights:
        copy.wait()

    rest_of(1)
    forward(1)
    onward_b(3)
    arrived(2, 0, 0)
    arrived(2, 0, 1)
    along_b(2)
    backward(1)
    send_halves(1)

    rest_of(3)
    forward(3)
    onward_b(2)
    along_b(0)
    send_fulls(1)
    backward(3)
    send_halves(3)

    rest_of(2)
    forward(2)
    onward_b(0)
    settle(1)
    send_fulls(3)
    backward(2)
    send_halves(2)

    rest_of(0)
    forward(0)
    settle(3)
    send_fulls(2)
    backward(0)
    send_halves(0)

    weight_grad(2)
    settle(2)
    for k in range(2):
        last_half_copy(k).start()
    send_fulls(0)
    weight_grad(1)
    for k in range(2):
        last_half_copy(k).wait_recv()
        add_into(share(1 + 2 * k, 0, k), last_half.at[k])
        last_full_copy(k).start()
    weight_grad(3)
    settle(0)
    weight_grad(0)
    for k in range(2):
        last_full_copy(k).wait_recv()
    add_into(share(0, 0), last_full.at[0], last_full.at[1])
    input_out[...] = part[own, pl.ds(0, dim)]
    prob_out[...] = part[own, pl.ds(dim, LANES)]
    for k in range(2):
        ring_full_copy(k).wait_recv()
    weight_out[...] = weight_out[...] + ring_full[0].astype(F32) + ring_full[1].astype(F32)

    for da in range(4):
        for db in range(4):
            if da + db > 0:
                for h in range(2):
                    pass_on((da, db), (da, db), h, other).wait_send()
        give_copy(da).wait_send()
        for k in range(2):
            half_copy(da, k).wait_send()
            full_copy(da, k).wait_send()
    for k in range(2):
        last_half_copy(k).wait_send()
        last_full_copy(k).wait_send()
        ring_half_copy(k).wait_send()
        ring_full_copy(k).wait_send()


def body(activations, out_grad, combine_weights, expert_ids, gate_up_weight, down_weight):
    tok, dim = activations.shape
    hid = down_weight.shape[2]
    columns = jnp.arange(LANES, dtype=jnp.int32)
    named = expert_ids[:, :, None] == columns[None, None, :]
    table = jnp.sum(
        jnp.where(named, combine_weights.astype(F32)[:, :, None], 0.0), axis=1
    ).astype(BF16)
    feat = dim // 8
    dma = pltpu.SemaphoreType.DMA
    vmem = pltpu.VMEM
    wide = dim + LANES
    grad_input, probs, turned = pl.pallas_call(
        kernel,
        out_shape=(
            jax.ShapeDtypeStruct((tok, dim), BF16),
            jax.ShapeDtypeStruct((tok, LANES), BF16),
            jax.ShapeDtypeStruct((3 * hid, feat), F32),
        ),
        in_specs=[pl.BlockSpec(memory_space=pl.ANY)] * 5,
        out_specs=[pl.BlockSpec(memory_space=pltpu.VMEM)] * 3,
        scratch_shapes=[
            vmem((16 * tok, 2 * dim + LANES), BF16),
            vmem((dim, 2 * hid), BF16),
            vmem((dim, hid), BF16),
            vmem((3 * hid, 16 * tok), BF16),
            vmem((4 * tok, 2 * hid), BF16),
            vmem((16 * tok, wide), BF16),
            vmem((4, 2, tok // 2, wide), BF16),
            vmem((4, 2, tok, wide), BF16),
            vmem((2, tok // 2, wide), BF16),
            vmem((2, tok, wide), BF16),
            vmem((4, 3 * hid, feat), BF16),
            vmem((4, 3 * hid, feat), BF16),
            vmem((2, 3 * hid // 2, feat), BF16),
            vmem((2, 3 * hid, feat), BF16),
            dma((5,)),
            dma((4, 4, 2)), dma((4, 4, 2)),
            dma((4, 2)), dma((4, 2)), dma((4, 2)), dma((4, 2)),
            dma((2,)), dma((2,)), dma((2,)), dma((2,)),
            dma((4,)), dma((4,)), dma((2,)), dma((2,)), dma((2,)), dma((2,)),
        ],
        compiler_params=pltpu.CompilerParams(
            collective_id=0, has_side_effects=True, vmem_limit_bytes=67043328
        ),
        name="routed",
    )(activations, out_grad, table, gate_up_weight[0], down_weight[0])
    grad_combine = jnp.sum(
        jnp.where(named, probs.astype(F32)[:, None, :], 0.0), axis=2
    ).astype(BF16)
    return (grad_input, grad_combine, turned[: 2 * hid].T[None], turned[2 * hid :].T[None])


def solution(mesh):
    rows = P(("expert", "group"), None)
    return jax.shard_map(
        body,
        mesh=mesh,
        in_specs=(rows, rows, rows, rows, P("expert", None, None), P("expert", None, None)),
        out_specs=(rows, rows, P("expert", "group", None), P("expert", "group", None)),
        check_vma=False,
    )
```

```python
import functools

import jax
import jax.numpy as jnp
from jax import lax
from jax.experimental import pallas as pl
from jax.experimental.pallas import tpu as pltpu
from jax.sharding import PartitionSpec as P

MESH = pl.DeviceIdType.MESH
LANES = 128
PLACE = {0: 0, 1: 1, 3: 2, 2: 3}
F32 = jnp.float32
BF16 = jnp.bfloat16


def kernel(
    x_in, g_in, ids_in, scale_in, gu_in, down_in,
    input_out, combine_out, gu_out, down_out,
    rows, weights, turned, pre_grad, part,
    cross_in, quarter_in, full_in, back_in,
    give, take, ring_half, ring_full, paired, block,
    local_sem, gather_send, gather_recv, weight_send, weight_recv,
    cross_send, cross_recv, quarter_send, quarter_recv, full_send, full_recv, back_send, back_recv,
    give_send, give_recv, ring_half_send, ring_half_recv, ring_full_send, ring_full_recv, pair_send, pair_recv,
):
    tok, dim = x_in.shape
    hid = down_in.shape[1]
    half, quarter = tok // 2, tok // 4
    tile = hid // 2
    feat = dim // 8
    e, q = lax.axis_index("expert"), lax.axis_index("group")
    z, x, y, c = e // 4, e % 4, q // 2, q % 2
    mate = (z + 1 - 2 * (z % 2)) * 4 + x
    expert = (e, mate)

    def dev_x(step):
        return (z * 4 + (x + step + 4) % 4, q)

    def dev_y(step):
        return (e, ((y + step + 4) % 4) * 2 + c)

    across = ((3 - z) * 4 + x, q)
    pair = (mate, q)
    other = (e, y * 2 + 1 - c)

    def remote(src, dst, send, recv, dev):
        return pltpu.make_async_remote_copy(
            src_ref=src, dst_ref=dst, send_sem=send, recv_sem=recv, device_id=dev, device_id_type=MESH
        )

    def place(zz, dx, h, s=None):
        start = PLACE[dx] * 2 * tok + zz * tok + h * half
        return pl.ds(start, half) if s is None else pl.ds(start + s * quarter, quarter)

    def token(src, dst, h, s, dev):
        k = 0 if s is None else s
        return remote(
            rows.at[place(*src, h, s), :], rows.at[place(*dst, h, s), :],
            gather_send.at[dst[0], dst[1], h, k], gather_recv.at[dst[0], dst[1], h, k], dev,
        )

    def arrived(zz, dx, h, s=None):
        token((zz, dx), (zz, dx), h, s, other).wait_recv()

    def along(zz, h):
        token((zz, 0), (zz, 1), h, None, dev_x(-1)).start()
        token((zz, 0), (zz, 3), h, None, dev_x(1)).start()

    def onward(zz, dx, h):
        s = dx // 2
        token((zz, dx), (zz, 2), h, s, dev_x(1 if s else -1)).start()

    def over(dx, h):
        token((0, dx), (1, dx), h, None, across).start()

    def weight_rows(dy, near, p):
        core = c if near == 0 else 1 - c
        start = (((y + dy) % 4) * 2 + core) * feat + p * (feat // 2)
        return pl.ds(pl.multiple_of(start, feat // 2), feat // 2)

    def weight(dy, dst, p, dev, origin=1):
        where = weight_rows(dy, 0, p)
        return remote(
            weights.at[origin, where, :], weights.at[1, where, :],
            weight_send.at[dst[0], dst[1], p], weight_recv.at[dst[0], dst[1], p], dev,
        )

    def weight_arrived(dy, near, p):
        where = weight_rows(dy, near, p)
        remote(
            weights.at[1, where, :], weights.at[1, where, :],
            weight_send.at[dy, near, p], weight_recv.at[dy, near, p], other,
        ).wait_recv()

    def weights_first():
        weight_arrived(0, 0, 0)
        weight(0, (1, 0), 0, dev_y(-1)).start()
        weight_arrived(0, 0, 1)
        weight(0, (3, 0), 1, dev_y(1)).start()
        weight(0, (1, 0), 1, dev_y(-1)).start()
        weight(0, (3, 0), 0, dev_y(1)).start()
        for p in range(2):
            weight(0, (0, 1), p, other).start()

    def weights_second():
        weight_arrived(1, 0, 0)
        weight(1, (2, 0), 0, dev_y(-1)).start()
        weight_arrived(3, 0, 1)
        weight(3, (2, 0), 1, dev_y(1)).start()
        weight(1, (1, 1), 0, other).start()
        weight(3, (3, 1), 1, other).start()

    def weights_third():
        weight_arrived(1, 0, 1)
        weight(1, (1, 1), 1, other).start()
        weight_arrived(3, 0, 0)
        weight(3, (3, 1), 0, other).start()
        for p in range(2):
            weight_arrived(2, 0, p)
            weight(2, (2, 1), p, other).start()

    def weights_last():
        for dy in range(4):
            for p in range(2):
                weight_arrived(dy, 1, p)

    STREAMS = ((0, 1), (0, 0), (1, 0))

    def add_into(dst, *srcs):
        total = dst[...].astype(F32)
        for src in srcs:
            total = total + src[...].astype(F32)
        dst[...] = total.astype(dst.dtype)

    def cross_copy(dx):
        return remote(
            part.at[place(1, dx, 1), :], cross_in.at[PLACE[dx]], cross_send.at[dx], cross_recv.at[dx], across
        )

    def quarter_copy(n, s):
        zz, h = STREAMS[n]
        return remote(
            part.at[place(zz, 2, h, s), :], quarter_in.at[n, s],
            quarter_send.at[n, s], quarter_recv.at[n, s], dev_x(-1 if s else 1),
        )

    def full_copy(n, s):
        zz, h = STREAMS[n]
        return remote(
            part.at[place(zz, 3 if s else 1, h), :], full_in.at[n, s],
            full_send.at[n, s], full_recv.at[n, s], dev_x(-1 if s else 1),
        )

    def back_copy():
        return remote(part.at[place(1, 0, 0), :], back_in, back_send.at[0], back_recv.at[0], across)

    def crossed(dx):
        cross_copy(dx).wait_recv()
        add_into(part.at[place(0, dx, 1), :], cross_in.at[PLACE[dx]])

    def send_quarters(n):
        for s in range(2):
            quarter_copy(n, s).start()

    def send_fulls(n):
        zz, h = STREAMS[n]
        for s in range(2):
            quarter_copy(n, s).wait_recv()
            add_into(part.at[place(zz, 3 if s else 1, h, s), :], quarter_in.at[n, s])
            full_copy(n, s).start()

    def settle(n):
        zz, h = STREAMS[n]
        for s in range(2):
            full_copy(n, s).wait_recv()
        add_into(part.at[place(zz, 0, h), :], full_in.at[n, 0], full_in.at[n, 1])

    def forward(k, r0, count):
        lane = lax.broadcasted_iota(jnp.int32, (count, LANES), 1)
        table = rows[pl.ds(r0, count), pl.ds(2 * dim, LANES)].astype(F32)
        scale = jnp.sum(jnp.where(lane == expert[k], table, 0.0), axis=1, keepdims=True)

        def step(n, prob):
            n0 = pl.multiple_of(n * tile, tile)
            n1 = pl.multiple_of(hid + n * tile, tile)
            n2 = pl.multiple_of(2 * hid + n * tile, tile)
            xs = rows[pl.ds(r0, count), pl.ds(0, dim)]
            gate = jnp.dot(xs, weights[k, :, pl.ds(n0, tile)], preferred_element_type=F32)
            upper = jnp.dot(xs, weights[k, :, pl.ds(n1, tile)], preferred_element_type=F32)
            raw = jnp.dot(
                rows[pl.ds(r0, count), pl.ds(dim, dim)], weights[k, :, pl.ds(n2, tile)], preferred_element_type=F32
            )
            sig = jax.nn.sigmoid(gate)
            silu = gate * sig
            hidden = (silu * upper).astype(BF16).astype(F32)
            grad = raw * scale
            gate_grad = (grad * upper * sig * (1.0 + gate * (1.0 - sig))).astype(BF16)
            upper_grad = (grad * silu).astype(BF16)
            pre_grad[k, pl.ds(r0, count), pl.ds(n0, tile)] = gate_grad
            pre_grad[k, pl.ds(r0, count), pl.ds(n1, tile)] = upper_grad
            turned[k, pl.ds(n0, tile), pl.ds(r0, count)] = gate_grad.T
            turned[k, pl.ds(n1, tile), pl.ds(r0, count)] = upper_grad.T
            turned[k, pl.ds(n2, tile), pl.ds(r0, count)] = (hidden * scale).astype(BF16).T
            return prob + jnp.sum(hidden * raw, axis=1, keepdims=True)

        prob = lax.fori_loop(0, 2, step, jnp.zeros((count, 1), F32))
        mine = jnp.where(lane == expert[k], prob, 0.0).astype(BF16)
        if k == 0:
            part[pl.ds(r0, count), pl.ds(dim, LANES)] = mine
        else:
            part[pl.ds(r0, count), pl.ds(dim, LANES)] = part[pl.ds(r0, count), pl.ds(dim, LANES)] + mine

    def backward(r0, count):
        wide = dim // 4

        @pl.loop(0, 4)
        def _(m):
            m0 = pl.multiple_of(m * wide, wide)
            total = None
            for k in range(2):
                term = lax.dot_general(
                    pre_grad[k, pl.ds(r0, count), :], weights[k, pl.ds(m0, wide), pl.ds(0, 2 * hid)],
                    (((1,), (1,)), ((), ())), preferred_element_type=F32,
                )
                total = term if total is None else total + term
            part[pl.ds(r0, count), pl.ds(m0, wide)] = total.astype(BF16)

    def weight_block(k, dy, core, put):
        f0 = (((y + dy) % 4) * 2 + core) * feat

        @pl.loop(0, 3)
        def _(i):
            i0 = pl.multiple_of(i * hid, hid)
            lane = pl.multiple_of(f0 + dim * (i // 2), feat)
            put(i0, jnp.dot(turned[k, pl.ds(i0, hid), :], rows[:, pl.ds(lane, feat)], preferred_element_type=F32))

    def give_copy(k, dy):
        return remote(give.at[k, dy], take.at[k, dy], give_send.at[k, dy], give_recv.at[k, dy], other)

    high = 3 * hid // 2

    def ring_half_copy(k, s):
        return remote(
            take.at[k, 2, pl.ds(s * high, high), :], ring_half.at[k, s],
            ring_half_send.at[k, s], ring_half_recv.at[k, s], dev_y(-1 if s else 1),
        )

    def ring_full_copy(k, s):
        return remote(
            take.at[k, 3 if s else 1], ring_full.at[k, s],
            ring_full_send.at[k, s], ring_full_recv.at[k, s], dev_y(-1 if s else 1),
        )

    def pair_copy():
        return remote(take.at[1, 0], paired, pair_send.at[0], pair_recv.at[0], pair)

    def weight_grad(k, dy):
        def put_give(i0, value):
            give[k, dy, pl.ds(i0, hid), :] = value.astype(BF16)

        weight_block(k, dy, 1 - c, put_give)
        give_copy(k, dy).start()

        def put_own(i0, value):
            block[pl.ds(i0, hid), :] = value

        weight_block(k, dy, c, put_own)
        give_copy(k, dy).wait_recv()
        if k == 0 and dy == 0:
            block[...] = block[...] + take[0, 0].astype(F32)
            return
        take[k, dy] = (block[...] + take[k, dy].astype(F32)).astype(BF16)
        if dy == 2:
            for s in range(2):
                ring_half_copy(k, s).start()
        elif dy != 0:
            s = dy // 2
            ring_half_copy(k, s).wait_recv()
            add_into(take.at[k, dy, pl.ds(s * high, high), :], ring_half.at[k, s])
            ring_full_copy(k, s).start()

    own = pl.ds(0, tok)
    mine = [
        pltpu.make_async_copy(x_in, rows.at[own, pl.ds(0, dim)], local_sem.at[0]),
        pltpu.make_async_copy(g_in, rows.at[own, pl.ds(dim, dim)], local_sem.at[1]),
    ]
    loads = [
        pltpu.make_async_copy(gu_in, weights.at[0, :, pl.ds(0, 2 * hid)], local_sem.at[2]),
        pltpu.make_async_copy(down_in, weights.at[0, :, pl.ds(2 * hid, hid)], local_sem.at[3]),
    ]
    for copy in mine + loads:
        copy.start()
    barrier = pltpu.get_barrier_semaphore()
    for dev in (dev_x(1), dev_x(-1), dev_y(1), dev_y(-1), across, pair, other):
        pl.semaphore_signal(barrier, inc=1, device_id=dev, device_id_type=MESH)
    lanes = lax.broadcasted_iota(jnp.int32, (tok, LANES), 1)
    table = jnp.zeros((tok, LANES), F32)
    for k in range(ids_in.shape[1]):
        table = table + jnp.where(lanes == ids_in[:, k : k + 1], scale_in[:, k : k + 1].astype(F32), 0.0)
    rows[own, pl.ds(2 * dim, LANES)] = table.astype(BF16)
    pl.semaphore_wait(barrier, 7)
    for copy in mine:
        copy.wait()

    along(0, 1)
    over(0, 0)
    along(0, 0)
    over(0, 1)
    for copy in loads:
        copy.wait()
    for p in range(2):
        weight(0, (0, 0), p, pair, origin=0).start()
    for dx in (1, 3):
        arrived(0, dx, 1)
        onward(0, dx, 1)
        over(dx, 1)
    arrived(1, 0, 0)
    along(1, 0)
    weights_first()
    for dx in (1, 3):
        arrived(0, dx, 0)
        onward(0, dx, 0)
    arrived(0, 2, 1, 0)
    arrived(0, 2, 1, 1)
    over(2, 1)
    weights_second()
    for dx in (1, 3):
        arrived(1, dx, 0)
        onward(1, dx, 0)
    arrived(1, 0, 1)
    arrived(1, 1, 1)

    two = 2 * tok
    forward(0, 0, 2 * two)
    weights_third()
    arrived(1, 3, 1)
    forward(0, 2 * two, two)
    weights_last()
    forward(1, 0, 2 * two)
    forward(1, 2 * two, two)
    arrived(1, 2, 1)
    for s in range(2):
        arrived(0, 2, 0, s)
        arrived(1, 2, 0, s)
    for k in range(2):
        forward(k, 3 * two, two)

    weight_grad(1, 2)
    backward(3 * two, two)
    cross_copy(2).start()
    send_quarters(1)
    send_quarters(2)
    weight_grad(1, 1)
    backward(2 * two, two)
    cross_copy(3).start()
    crossed(2)
    send_quarters(0)
    weight_grad(1, 3)
    backward(0, 2 * two)
    cross_copy(1).start()
    cross_copy(0).start()
    send_fulls(2)
    send_fulls(1)
    weight_grad(1, 0)
    crossed(3)
    crossed(1)
    send_fulls(0)
    settle(2)
    back_copy().start()
    weight_grad(0, 2)
    weight_grad(0, 1)
    settle(1)
    weight_grad(0, 3)
    for s in range(2):
        ring_full_copy(1, s).wait_recv()
    add_into(take.at[1, 0], ring_full.at[1, 0], ring_full.at[1, 1])
    pair_copy().start()
    crossed(0)
    settle(0)
    weight_grad(0, 0)
    back_copy().wait_recv()
    add_into(part.at[place(0, 0, 0), :], back_in)
    input_out[...] = part[own, pl.ds(0, dim)]
    probs = part[own, pl.ds(dim, LANES)].astype(F32)
    for k in range(ids_in.shape[1]):
        picked = jnp.where(lanes == ids_in[:, k : k + 1], probs, 0.0)
        combine_out[:, k : k + 1] = jnp.sum(picked, axis=1, keepdims=True).astype(BF16)
    for s in range(2):
        ring_full_copy(0, s).wait_recv()
    pair_copy().wait_recv()
    total = block[...] + ring_full[0, 0].astype(F32) + ring_full[0, 1].astype(F32) + paired[...].astype(F32)
    gu_out[...] = total[: 2 * hid]
    down_out[...] = total[2 * hid :]

    sent = [(1, 0, 0, None), (1, 0, 1, None), (1, 1, 0, None), (1, 3, 0, None)]
    sent += [(0, dx, h, None) for dx in (1, 3) for h in range(2)]
    sent += [(1, dx, 1, None) for dx in (1, 2, 3)]
    sent += [(zz, 2, h, s) for zz, h in STREAMS for s in range(2)]
    for zz, dx, h, s in sent:
        token((zz, dx), (zz, dx), h, s, other).wait_send()
    for dy in range(4):
        for near in range(2):
            for p in range(2):
                weight(0, (dy, near), p, other).wait_send()
        cross_copy(dy).wait_send()
        for k in range(2):
            give_copy(k, dy).wait_send()
    for s in range(2):
        for n in range(3):
            quarter_copy(n, s).wait_send()
            full_copy(n, s).wait_send()
        for k in range(2):
            ring_half_copy(k, s).wait_send()
            ring_full_copy(k, s).wait_send()
    back_copy().wait_send()
    pair_copy().wait_send()


def body(activations, out_grad, combine_weights, expert_ids, gate_up_weight, down_weight):
    tok, dim = activations.shape
    top = expert_ids.shape[1]
    hid = down_weight.shape[2]
    feat = dim // 8
    dma = pltpu.SemaphoreType.DMA
    vmem = pltpu.VMEM
    wide = dim + LANES
    whole = pl.BlockSpec(memory_space=pltpu.VMEM)
    far = pl.BlockSpec(memory_space=pl.ANY)
    grad_input, grad_combine, grad_gu, grad_down = pl.pallas_call(
        kernel,
        out_shape=(
            jax.ShapeDtypeStruct((tok, dim), BF16),
            jax.ShapeDtypeStruct((tok, top), BF16),
            jax.ShapeDtypeStruct((2 * hid, feat), F32),
            jax.ShapeDtypeStruct((hid, feat), F32),
        ),
        in_specs=[far, far, whole, whole, far, far],
        out_specs=[whole] * 4,
        scratch_shapes=[
            vmem((8 * tok, 2 * dim + LANES), BF16),
            vmem((2, dim, 3 * hid), BF16),
            vmem((2, 3 * hid, 8 * tok), BF16),
            vmem((2, 8 * tok, 2 * hid), BF16),
            vmem((8 * tok, wide), BF16),
            vmem((4, tok // 2, wide), BF16),
            vmem((3, 2, tok // 4, wide), BF16),
            vmem((3, 2, tok // 2, wide), BF16),
            vmem((tok // 2, wide), BF16),
            vmem((2, 4, 3 * hid, feat), BF16),
            vmem((2, 4, 3 * hid, feat), BF16),
            vmem((2, 2, 3 * hid // 2, feat), BF16),
            vmem((2, 2, 3 * hid, feat), BF16),
            vmem((3 * hid, feat), BF16),
            vmem((3 * hid, feat), F32),
            dma((4,)),
            dma((2, 4, 2, 2)), dma((2, 4, 2, 2)),
            dma((4, 2, 2)), dma((4, 2, 2)),
            dma((4,)), dma((4,)), dma((3, 2)), dma((3, 2)), dma((3, 2)), dma((3, 2)), dma((1,)), dma((1,)),
            dma((2, 4)), dma((2, 4)), dma((2, 2)), dma((2, 2)), dma((2, 2)), dma((2, 2)), dma((1,)), dma((1,)),
        ],
        compiler_params=pltpu.CompilerParams(
            collective_id=0, has_side_effects=True, vmem_limit_bytes=67043328
        ),
        name="routed",
    )(activations, out_grad, expert_ids, combine_weights, gate_up_weight[0], down_weight[0])
    return (grad_input, grad_combine, grad_gu.T[None], grad_down.T[None])


def solution(mesh):
    rows = P(("expert", "group"), None)
    return jax.shard_map(
        body,
        mesh=mesh,
        in_specs=(rows, rows, rows, rows, P("expert", None, None), P("expert", None, None)),
        out_specs=(rows, rows, P("expert", "group", None), P("expert", "group", None)),
        check_vma=False,
    )
```

```python
import functools

import jax
import jax.numpy as jnp
from jax import lax
from jax.experimental import pallas as pl
from jax.experimental.pallas import tpu as pltpu
from jax.sharding import PartitionSpec as P

MESH = pl.DeviceIdType.MESH
LANES = 128
PLACE = {0: 0, 1: 1, 3: 2, 2: 3}
F32 = jnp.float32
BF16 = jnp.bfloat16


def kernel(
    x_in, g_in, ids_in, scale_in, gu_in, down_in,
    input_out, combine_out, gu_out, down_out,
    rows, weights, turned, pre_grad, part,
    cross_in, quarter_in, full_in, back_in,
    give, take, ring_half, ring_full, early, paired, block,
    local_sem, gather_send, gather_recv, weight_send, weight_recv,
    cross_send, cross_recv, quarter_send, quarter_recv, full_send, full_recv, back_send, back_recv,
    give_send, give_recv, ring_half_send, ring_half_recv, ring_full_send, ring_full_recv,
    early_send, early_recv, pair_send, pair_recv,
):
    tok, dim = x_in.shape
    hid = down_in.shape[1]
    half, quarter = tok // 2, tok // 4
    tile = hid // 2
    feat = dim // 8
    e, q = lax.axis_index("expert"), lax.axis_index("group")
    z, x, y, c = e // 4, e % 4, q // 2, q % 2
    mate = (z + 1 - 2 * (z % 2)) * 4 + x
    expert = (e, mate)

    def dev_x(step):
        return (z * 4 + (x + step + 4) % 4, q)

    def dev_y(step):
        return (e, ((y + step + 4) % 4) * 2 + c)

    across = ((3 - z) * 4 + x, q)
    pair = (mate, q)
    other = (e, y * 2 + 1 - c)

    def remote(src, dst, send, recv, dev):
        return pltpu.make_async_remote_copy(
            src_ref=src, dst_ref=dst, send_sem=send, recv_sem=recv, device_id=dev, device_id_type=MESH
        )

    def place(zz, dx, h, s=None):
        start = PLACE[dx] * 2 * tok + zz * tok + h * half
        return pl.ds(start, half) if s is None else pl.ds(start + s * quarter, quarter)

    def token(src, dst, h, s, dev):
        k = 0 if s is None else s
        return remote(
            rows.at[place(*src, h, s), :], rows.at[place(*dst, h, s), :],
            gather_send.at[dst[0], dst[1], h, k], gather_recv.at[dst[0], dst[1], h, k], dev,
        )

    def arrived(zz, dx, h, s=None):
        token((zz, dx), (zz, dx), h, s, other).wait_recv()

    def along(zz, h):
        token((zz, 0), (zz, 1), h, None, dev_x(-1)).start()
        token((zz, 0), (zz, 3), h, None, dev_x(1)).start()

    def onward(zz, dx, h):
        s = dx // 2
        token((zz, dx), (zz, 2), h, s, dev_x(1 if s else -1)).start()

    def over(dx, h):
        token((0, dx), (1, dx), h, None, across).start()

    def weight_rows(dy, near, p):
        core = c if near == 0 else 1 - c
        start = (((y + dy) % 4) * 2 + core) * feat + p * (feat // 2)
        return pl.ds(pl.multiple_of(start, feat // 2), feat // 2)

    def weight(dy, dst, p, dev, origin=1):
        where = weight_rows(dy, 0, p)
        return remote(
            weights.at[origin, where, :], weights.at[1, where, :],
            weight_send.at[dst[0], dst[1], p], weight_recv.at[dst[0], dst[1], p], dev,
        )

    def weight_arrived(dy, near, p):
        where = weight_rows(dy, near, p)
        remote(
            weights.at[1, where, :], weights.at[1, where, :],
            weight_send.at[dy, near, p], weight_recv.at[dy, near, p], other,
        ).wait_recv()

    def weights_first():
        weight_arrived(0, 0, 0)
        weight(0, (1, 0), 0, dev_y(-1)).start()
        weight_arrived(0, 0, 1)
        weight(0, (3, 0), 1, dev_y(1)).start()
        weight(0, (1, 0), 1, dev_y(-1)).start()
        weight(0, (3, 0), 0, dev_y(1)).start()
        for p in range(2):
            weight(0, (0, 1), p, other).start()

    def weights_second():
        weight_arrived(1, 0, 0)
        weight(1, (2, 0), 0, dev_y(-1)).start()
        weight_arrived(3, 0, 1)
        weight(3, (2, 0), 1, dev_y(1)).start()
        weight(1, (1, 1), 0, other).start()
        weight(3, (3, 1), 1, other).start()

    def weights_third():
        weight_arrived(1, 0, 1)
        weight(1, (1, 1), 1, other).start()
        weight_arrived(3, 0, 0)
        weight(3, (3, 1), 0, other).start()
        for p in range(2):
            weight_arrived(2, 0, p)
            weight(2, (2, 1), p, other).start()

    def weights_last():
        for dy in range(4):
            for p in range(2):
                weight_arrived(dy, 1, p)

    STREAMS = ((0, 1), (0, 0), (1, 0))

    def add_into(dst, *srcs):
        total = dst[...].astype(F32)
        for src in srcs:
            total = total + src[...].astype(F32)
        dst[...] = total.astype(dst.dtype)

    def cross_copy(dx):
        return remote(
            part.at[place(1, dx, 1), :], cross_in.at[PLACE[dx]], cross_send.at[dx], cross_recv.at[dx], across
        )

    def quarter_copy(n, s):
        zz, h = STREAMS[n]
        return remote(
            part.at[place(zz, 2, h, s), :], quarter_in.at[n, s],
            quarter_send.at[n, s], quarter_recv.at[n, s], dev_x(-1 if s else 1),
        )

    def full_copy(n, s):
        zz, h = STREAMS[n]
        return remote(
            part.at[place(zz, 3 if s else 1, h), :], full_in.at[n, s],
            full_send.at[n, s], full_recv.at[n, s], dev_x(-1 if s else 1),
        )

    def back_copy():
        return remote(part.at[place(1, 0, 0), :], back_in, back_send.at[0], back_recv.at[0], across)

    def crossed(dx):
        cross_copy(dx).wait_recv()
        add_into(part.at[place(0, dx, 1), :], cross_in.at[PLACE[dx]])

    def send_quarters(n):
        for s in range(2):
            quarter_copy(n, s).start()

    def send_fulls(n):
        zz, h = STREAMS[n]
        for s in range(2):
            quarter_copy(n, s).wait_recv()
            add_into(part.at[place(zz, 3 if s else 1, h, s), :], quarter_in.at[n, s])
            full_copy(n, s).start()

    def settle(n):
        zz, h = STREAMS[n]
        for s in range(2):
            full_copy(n, s).wait_recv()
        add_into(part.at[place(zz, 0, h), :], full_in.at[n, 0], full_in.at[n, 1])

    def forward(k, r0, count):
        lane = lax.broadcasted_iota(jnp.int32, (count, LANES), 1)
        table = rows[pl.ds(r0, count), pl.ds(2 * dim, LANES)].astype(F32)
        scale = jnp.sum(jnp.where(lane == expert[k], table, 0.0), axis=1, keepdims=True)

        def step(n, prob):
            n0 = pl.multiple_of(n * tile, tile)
            n1 = pl.multiple_of(hid + n * tile, tile)
            n2 = pl.multiple_of(2 * hid + n * tile, tile)
            xs = rows[pl.ds(r0, count), pl.ds(0, dim)]
            gate = jnp.dot(xs, weights[k, :, pl.ds(n0, tile)], preferred_element_type=F32)
            upper = jnp.dot(xs, weights[k, :, pl.ds(n1, tile)], preferred_element_type=F32)
            raw = jnp.dot(
                rows[pl.ds(r0, count), pl.ds(dim, dim)], weights[k, :, pl.ds(n2, tile)], preferred_element_type=F32
            )
            sig = jax.nn.sigmoid(gate)
            silu = gate * sig
            hidden = (silu * upper).astype(BF16).astype(F32)
            grad = raw * scale
            gate_grad = (grad * upper * sig * (1.0 + gate * (1.0 - sig))).astype(BF16)
            upper_grad = (grad * silu).astype(BF16)
            pre_grad[k, pl.ds(r0, count), pl.ds(n0, tile)] = gate_grad
            pre_grad[k, pl.ds(r0, count), pl.ds(n1, tile)] = upper_grad
            turned[k, pl.ds(n0, tile), pl.ds(r0, count)] = gate_grad.T
            turned[k, pl.ds(n1, tile), pl.ds(r0, count)] = upper_grad.T
            turned[k, pl.ds(n2, tile), pl.ds(r0, count)] = (hidden * scale).astype(BF16).T
            return prob + jnp.sum(hidden * raw, axis=1, keepdims=True)

        prob = lax.fori_loop(0, 2, step, jnp.zeros((count, 1), F32))
        mine = jnp.where(lane == expert[k], prob, 0.0).astype(BF16)
        if k == 0:
            part[pl.ds(r0, count), pl.ds(dim, LANES)] = mine
        else:
            part[pl.ds(r0, count), pl.ds(dim, LANES)] = part[pl.ds(r0, count), pl.ds(dim, LANES)] + mine

    def backward(r0, count):
        wide = dim // 4

        @pl.loop(0, 4)
        def _(m):
            m0 = pl.multiple_of(m * wide, wide)
            total = None
            for k in range(2):
                term = lax.dot_general(
                    pre_grad[k, pl.ds(r0, count), :], weights[k, pl.ds(m0, wide), pl.ds(0, 2 * hid)],
                    (((1,), (1,)), ((), ())), preferred_element_type=F32,
                )
                total = term if total is None else total + term
            part[pl.ds(r0, count), pl.ds(m0, wide)] = total.astype(BF16)

    def weight_block(k, dy, core, put):
        f0 = (((y + dy) % 4) * 2 + core) * feat

        @pl.loop(0, 3)
        def _(i):
            i0 = pl.multiple_of(i * hid, hid)
            lane = pl.multiple_of(f0 + dim * (i // 2), feat)
            put(i0, jnp.dot(turned[k, pl.ds(i0, hid), :], rows[:, pl.ds(lane, feat)], preferred_element_type=F32))

    def give_copy(k, dy):
        return remote(give.at[k, dy], take.at[k, dy], give_send.at[k, dy], give_recv.at[k, dy], other)

    high = 3 * hid // 2

    def part_of(k, dy, s):
        return take.at[k, dy, pl.ds(s * high, high), :]

    def ring_half_copy(s):
        return remote(
            part_of(0, 2, s), ring_half.at[s], ring_half_send.at[s], ring_half_recv.at[s], dev_y(-1 if s else 1)
        )

    def ring_full_copy(k, s, h):
        return remote(
            part_of(k, 3 if s else 1, h), ring_full.at[k, s, pl.ds(h * high, high), :],
            ring_full_send.at[k, s, h], ring_full_recv.at[k, s, h], dev_y(-1 if s else 1),
        )

    def early_copy(s):
        return remote(part_of(1, 2, s), early.at[s], early_send.at[s], early_recv.at[s], pair)

    def pair_copy(s):
        return remote(
            part_of(1, 0, s), paired.at[pl.ds(s * high, high), :], pair_send.at[s], pair_recv.at[s], pair
        )

    def give_block(k, dy):
        def put(i0, value):
            give[k, dy, pl.ds(i0, hid), :] = value.astype(BF16)

        weight_block(k, dy, 1 - c, put)
        give_copy(k, dy).start()

    def own_block(k, dy):
        give_copy(k, dy).wait_recv()

        def put(i0, value):
            value = value + take[k, dy, pl.ds(i0, hid), :].astype(F32)
            if k == 0 and dy == 0:
                block[pl.ds(i0, hid), :] = value
            else:
                take[k, dy, pl.ds(i0, hid), :] = value.astype(BF16)

        weight_block(k, dy, c, put)

    own = pl.ds(0, tok)
    mine = [
        pltpu.make_async_copy(x_in, rows.at[own, pl.ds(0, dim)], local_sem.at[0]),
        pltpu.make_async_copy(g_in, rows.at[own, pl.ds(dim, dim)], local_sem.at[1]),
    ]
    loads = [
        pltpu.make_async_copy(gu_in, weights.at[0, :, pl.ds(0, 2 * hid)], local_sem.at[2]),
        pltpu.make_async_copy(down_in, weights.at[0, :, pl.ds(2 * hid, hid)], local_sem.at[3]),
    ]
    for copy in mine + loads:
        copy.start()
    barrier = pltpu.get_barrier_semaphore()
    for dev in (dev_x(1), dev_x(-1), dev_y(1), dev_y(-1), across, pair, other):
        pl.semaphore_signal(barrier, inc=1, device_id=dev, device_id_type=MESH)
    lanes = lax.broadcasted_iota(jnp.int32, (tok, LANES), 1)
    table = jnp.zeros((tok, LANES), F32)
    named = []
    for k in range(ids_in.shape[0]):
        named.append(jnp.broadcast_to(ids_in[k : k + 1, :], (LANES, tok)).T)
        scale = jnp.broadcast_to(scale_in[k : k + 1, :].astype(F32), (LANES, tok)).T
        table = table + jnp.where(lanes == named[k], scale, 0.0)
    rows[own, pl.ds(2 * dim, LANES)] = table.astype(BF16)
    pl.semaphore_wait(barrier, 7)
    for copy in mine:
        copy.wait()

    along(0, 1)
    over(0, 0)
    along(0, 0)
    over(0, 1)
    for copy in loads:
        copy.wait()
    for p in range(2):
        weight(0, (0, 0), p, pair, origin=0).start()
    for dx in (1, 3):
        arrived(0, dx, 1)
        onward(0, dx, 1)
        over(dx, 1)
    arrived(1, 0, 0)
    along(1, 0)
    weights_first()
    for dx in (1, 3):
        arrived(0, dx, 0)
        onward(0, dx, 0)
    arrived(0, 2, 1, 0)
    arrived(0, 2, 1, 1)
    over(2, 1)
    arrived(1, 0, 1)
    weights_second()
    forward(0, 0, 2 * tok)
    for dx in (1, 3):
        arrived(1, dx, 0)
        onward(1, dx, 0)
    arrived(1, 1, 1)

    two = 2 * tok
    forward(0, two, two)
    weights_third()
    weights_last()
    forward(1, 0, 2 * two)
    backward(0, 2 * two)
    for dx in (1, 0):
        cross_copy(dx).start()
    arrived(1, 3, 1)
    for k in range(2):
        forward(k, 2 * two, two)
    arrived(1, 2, 1)
    for s in range(2):
        arrived(0, 2, 0, s)
        arrived(1, 2, 0, s)
    for k in range(2):
        forward(k, 3 * two, two)

    give_block(1, 1)
    give_block(1, 3)
    own_block(1, 1)
    for h in range(2):
        ring_full_copy(1, 0, h).start()
    own_block(1, 3)
    for h in range(2):
        ring_full_copy(1, 1, h).start()
    give_block(1, 2)
    backward(3 * two, two)
    cross_copy(2).start()
    send_quarters(1)
    send_quarters(2)
    own_block(1, 2)
    for s in range(2):
        early_copy(s).start()
    give_block(0, 2)
    backward(2 * two, two)
    cross_copy(3).start()
    crossed(2)
    send_quarters(0)
    own_block(0, 2)
    give_block(0, 1)
    send_fulls(2)
    send_fulls(1)
    give_block(0, 3)
    own_block(0, 1)
    own_block(0, 3)
    for s in range(2):
        early_copy(s).wait_recv()
        add_into(part_of(0, 2, s), early.at[s])
        ring_half_copy(s).start()
        ring_full_copy(0, s, 1 - s).start()
    give_block(1, 0)
    crossed(3)
    crossed(1)
    send_fulls(0)
    settle(2)
    back_copy().start()
    own_block(1, 0)
    for h in range(2):
        for s in range(2):
            ring_full_copy(1, s, h).wait_recv()
        add_into(
            part_of(1, 0, h), ring_full.at[1, 0, pl.ds(h * high, high), :], ring_full.at[1, 1, pl.ds(h * high, high), :]
        )
        pair_copy(h).start()
    for s in range(2):
        ring_half_copy(s).wait_recv()
        add_into(part_of(0, 2 * s + 1, s), ring_half.at[s])
        ring_full_copy(0, s, s).start()
    give_block(0, 0)
    settle(1)
    crossed(0)
    settle(0)
    own_block(0, 0)
    back_copy().wait_recv()
    add_into(part.at[place(0, 0, 0), :], back_in)
    input_out[...] = part[own, pl.ds(0, dim)]
    probs = part[own, pl.ds(dim, LANES)].astype(F32)
    for k in range(ids_in.shape[0]):
        picked = jnp.sum(jnp.where(lanes == named[k], probs, 0.0), axis=1, keepdims=True)
        combine_out[k : k + 1, :] = jnp.broadcast_to(picked, (tok, LANES)).T[:1]
    for h in range(2):
        pair_copy(h).wait_recv()
    block[...] = block[...] + paired[...].astype(F32)
    for s in range(2):
        for h in range(2):
            ring_full_copy(0, s, h).wait_recv()
    total = block[...] + ring_full[0, 0].astype(F32) + ring_full[0, 1].astype(F32)
    gu_out[...] = total[: 2 * hid]
    down_out[...] = total[2 * hid :]

    sent = [(1, 0, 0, None), (1, 0, 1, None), (1, 1, 0, None), (1, 3, 0, None)]
    sent += [(0, dx, h, None) for dx in (1, 3) for h in range(2)]
    sent += [(1, dx, 1, None) for dx in (1, 2, 3)]
    sent += [(zz, 2, h, s) for zz, h in STREAMS for s in range(2)]
    for zz, dx, h, s in sent:
        token((zz, dx), (zz, dx), h, s, other).wait_send()
    for dy in range(4):
        for near in range(2):
            for p in range(2):
                weight(0, (dy, near), p, other).wait_send()
        cross_copy(dy).wait_send()
        for k in range(2):
            give_copy(k, dy).wait_send()
    for s in range(2):
        for n in range(3):
            quarter_copy(n, s).wait_send()
            full_copy(n, s).wait_send()
        ring_half_copy(s).wait_send()
        early_copy(s).wait_send()
        pair_copy(s).wait_send()
        for k in range(2):
            for h in range(2):
                ring_full_copy(k, s, h).wait_send()
    back_copy().wait_send()


def finish(input_in, combine_in, gu_in, down_in, input_out, combine_out, gu_out, down_out):
    input_out[...] = input_in[...]
    combine_out[...] = combine_in[...].astype(BF16)
    gu_out[...] = gu_in[...].T
    down_out[...] = down_in[...].T


def body(activations, out_grad, combine_weights, expert_ids, gate_up_weight, down_weight):
    tok, dim = activations.shape
    top = expert_ids.shape[1]
    hid = down_weight.shape[2]
    feat = dim // 8
    dma = pltpu.SemaphoreType.DMA
    vmem = pltpu.VMEM
    wide = dim + LANES
    whole = pl.BlockSpec(memory_space=pltpu.VMEM)
    far = pl.BlockSpec(memory_space=pl.ANY)
    grad_input, grad_combine, grad_gu, grad_down = pl.pallas_call(
        kernel,
        out_shape=(
            jax.ShapeDtypeStruct((tok, dim), BF16),
            jax.ShapeDtypeStruct((top, tok), F32),
            jax.ShapeDtypeStruct((2 * hid, feat), F32),
            jax.ShapeDtypeStruct((hid, feat), F32),
        ),
        in_specs=[far, far, whole, whole, far, far],
        out_specs=[whole] * 4,
        scratch_shapes=[
            vmem((8 * tok, 2 * dim + LANES), BF16),
            vmem((2, dim, 3 * hid), BF16),
            vmem((2, 3 * hid, 8 * tok), BF16),
            vmem((2, 8 * tok, 2 * hid), BF16),
            vmem((8 * tok, wide), BF16),
            vmem((4, tok // 2, wide), BF16),
            vmem((3, 2, tok // 4, wide), BF16),
            vmem((3, 2, tok // 2, wide), BF16),
            vmem((tok // 2, wide), BF16),
            vmem((2, 4, 3 * hid, feat), BF16),
            vmem((2, 4, 3 * hid, feat), BF16),
            vmem((2, 3 * hid // 2, feat), BF16),
            vmem((2, 2, 3 * hid, feat), BF16),
            vmem((2, 3 * hid // 2, feat), BF16),
            vmem((3 * hid, feat), BF16),
            vmem((3 * hid, feat), F32),
            dma((4,)),
            dma((2, 4, 2, 2)), dma((2, 4, 2, 2)),
            dma((4, 2, 2)), dma((4, 2, 2)),
            dma((4,)), dma((4,)), dma((3, 2)), dma((3, 2)), dma((3, 2)), dma((3, 2)), dma((1,)), dma((1,)),
            dma((2, 4)), dma((2, 4)), dma((2,)), dma((2,)), dma((2, 2, 2)), dma((2, 2, 2)),
            dma((2,)), dma((2,)), dma((2,)), dma((2,)),
        ],
        compiler_params=pltpu.CompilerParams(
            collective_id=0, has_side_effects=True, vmem_limit_bytes=67043328
        ),
        name="routed",
    )(activations, out_grad, expert_ids.T, combine_weights.T, gate_up_weight[0], down_weight[0])
    grad_input, grad_combine, grad_gu, grad_down = pl.pallas_call(
        finish,
        out_shape=(
            jax.ShapeDtypeStruct((tok, dim), BF16),
            jax.ShapeDtypeStruct((top, tok), BF16),
            jax.ShapeDtypeStruct((feat, 2 * hid), F32),
            jax.ShapeDtypeStruct((feat, hid), F32),
        ),
        in_specs=[whole] * 4,
        out_specs=[whole] * 4,
        name="finish",
    )(grad_input, grad_combine, grad_gu, grad_down)
    return (grad_input, grad_combine.T, grad_gu[None], grad_down[None])


def solution(mesh):
    rows = P(("expert", "group"), None)
    return jax.shard_map(
        body,
        mesh=mesh,
        in_specs=(rows, rows, rows, rows, P("expert", None, None), P("expert", None, None)),
        out_specs=(rows, rows, P("expert", "group", None), P("expert", "group", None)),
        check_vma=False,
    )
```
